32 devices in a mesh: grp: 2 (over x), seq: 8 (over z, y), ten: 2 (over core).
Axes of the slice: x: 2, y: 2, z: 4, core: 2. Of those that a mesh axis runs over, the one named last changes fastest.
Arguments:
- queries: bfloat16 [1024, 4096], P(('grp', 'seq'), 'ten'), parts along dimension 0, may hold values from -128 to 128
- keys: bfloat16 [1024, 512], P(('grp', 'seq'), 'ten'), parts along dimension 0, may hold values from -6 to 6
- values: bfloat16 [1024, 512], P(('grp', 'seq'), 'ten'), parts along dimension 0, may hold values from -6 to 6
- hidden: bfloat16 [1024, 8192], P(('grp', 'seq')), parts along dimension 0, may hold values from -6 to 6
- norm_gain: float32 [8192], replicated, may hold values from 0.1 to 1.9
- retained_lists: int32 [1024], P(('grp', 'seq')), parts along dimension 0, may hold values from -1 to 63, as said below
- counts: int32 [16], P('grp'), parts along dimension 0, may hold values from 0 to 64, as said below
- affine_matrix: bfloat16 [8192, 5120], P('seq', 'ten'), may hold values from -0.0625 to 0.0625
- affine_offset_vector: float32 [5120], P('ten'), may hold values from -3 to 3
Outputs:
- context: float32 [1024, 4096], P(('grp', 'seq'), 'ten'), parts along dimension 0
- col_scores: float32 [1024], P(('grp', 'seq')), parts along dimension 0
- tier_third_mapped_triples: float32 [512, 5120], P(('grp', 'seq'), 'ten'), parts along dimension 0
The draws below stay inside these ranges and needn't reach their ends.
There are 2 independent parts, one for each index of `grp`. The reference program is written for one: setup_inputs(seed, part) draws one part's arguments, and reference() takes and returns one part's arrays. A program takes and returns all parts, laid end to end along the dimension named above; an argument that names none is the same for every part. Nothing has to cross between parts.
Inputs may be any that keep to these rules, and one draw needn't show every extreme that they name: `retained_lists`: entries s*64 to (s+1)*64 - 1 hold, in their first counts[s] places, the kept local rows of shard s in rising order, and -1 after them. counts sum to 256; some shard keeps all its 64 rows.
All inputs are finite; a program needn't handle non-finite values.
Results may differ from the reference program's by a relative error of at most 0.0027.
Values may be sent and summed in bfloat16 or wider, within the bound.
A program may use at most 64 MiB of HBM per device.

```python
import math
import jax
import jax.numpy as jnp
from jax import lax

D = 8192
HEAD_SIZE = 128
QUERY_HEADS = 32
KEY_VALUE_HEADS = 4
QD = 64
QUERY_BLOCK_ROWS = 512
QKVW = 5120


def paired_draw(key):
    queries = jnp.clip(jax.random.normal(jax.random.fold_in(key, 101), (QUERY_BLOCK_ROWS, QUERY_HEADS * HEAD_SIZE), jnp.float32), -6.0, 6.0)
    keys = jnp.clip(jax.random.normal(jax.random.fold_in(key, 202), (QUERY_BLOCK_ROWS, KEY_VALUE_HEADS * HEAD_SIZE), jnp.float32), -6.0, 6.0)
    head_place = jnp.arange(QUERY_HEADS, dtype=jnp.float32) / max(QUERY_HEADS - 1, 1)
    jitter = jax.random.uniform(jax.random.fold_in(key, 505), (QUERY_HEADS,), jnp.float32, 0.85, 1.15)
    head_scale = 0.6 * jnp.exp(head_place * math.log(6.0)) * jitter
    queries = queries * jnp.repeat(head_scale, HEAD_SIZE)[None, :]
    queries = jnp.clip(queries, -128.0, 128.0)
    return (queries, keys)


def draw_queries(key, part):
    return paired_draw(key)[0].astype(jnp.bfloat16)


def draw_keys(key, part):
    return paired_draw(key)[1].astype(jnp.bfloat16)


def retained_sequence_pick(key):
    base = jax.random.fold_in(key, 404)
    shard_count = QUERY_BLOCK_ROWS // QD
    levels = jax.random.randint(jax.random.fold_in(base, 1), (shard_count,), 0, 4)
    full_shard = jax.random.randint(jax.random.fold_in(base, 2), (), 0, shard_count)
    levels = jnp.where(jnp.arange(shard_count, dtype=jnp.int32) == full_shard, 5, levels)
    noise = jax.random.randint(jax.random.fold_in(base, 3), (QUERY_BLOCK_ROWS,), 0, 1024)
    position = jnp.arange(QUERY_BLOCK_ROWS, dtype=jnp.int32)
    ranking = (jnp.repeat(levels, QD) * 1024 + noise) * QUERY_BLOCK_ROWS + position
    unused, picked = lax.top_k(ranking, QUERY_BLOCK_ROWS // 2)
    marked = jnp.zeros((QUERY_BLOCK_ROWS,), jnp.int32).at[picked].set(1).reshape(shard_count, QD)
    counts = jnp.sum(marked, axis=1).astype(jnp.int32)
    partition_inner_position = jnp.arange(QD, dtype=jnp.int32)
    order_key = (1 - marked) * QD + partition_inner_position[None, :]
    ordered = jnp.argsort(order_key, axis=1, stable=True).astype(jnp.int32)
    retained_lists = jnp.where(partition_inner_position[None, :] < counts[:, None], ordered, -1).reshape(QUERY_BLOCK_ROWS)
    return (retained_lists, counts)


def draw_retained_lists(key, part):
    return retained_sequence_pick(key)[0]


def draw_counts(key, part):
    return retained_sequence_pick(key)[1]


def shard_levels(stream_key, dims, split, smallest, largest):
    level, own = 1.0, jax.random.fold_in(stream_key, 6)
    for axis_at, blocks in split:
        heights = jnp.exp(jax.random.uniform(jax.random.fold_in(own, axis_at), (blocks,), jnp.float32, smallest / len(split), largest / len(split)))
        level = level * jnp.repeat(heights, dims[axis_at] // blocks).reshape([-1 if axis == axis_at else 1 for axis in range(len(dims))])
    return level


def gaussian(rng, extent, width, limit, pieces=(), kind=jnp.bfloat16):
    entries = jax.random.normal(rng, extent, jnp.float32) * width
    if len(pieces) > 0:
        entries = shard_levels(rng, extent, pieces, -0.22, 0.18) * entries
    return jnp.clip(entries, min=-limit, max=limit).astype(kind)


def setup_inputs(seed: int = 0, part: int = 0) -> dict:
    arg_keys = jax.random.split(jax.random.key(seed), 10)
    part_keys = jax.random.split(jax.random.fold_in(arg_keys[9], part), 10)
    return {
        "queries": draw_queries(jax.random.fold_in(jax.random.fold_in(arg_keys[9], part), 71), part),
        "keys": draw_keys(jax.random.fold_in(jax.random.fold_in(arg_keys[9], part), 71), part),
        "values": gaussian(part_keys[2], (QUERY_BLOCK_ROWS, KEY_VALUE_HEADS * HEAD_SIZE), 1.0, 6.0, ((0, 8), (1, 2))),
        "hidden": gaussian(part_keys[3], (QUERY_BLOCK_ROWS, D), 1.0, 6.0, ((0, 8),)),
        "norm_gain": jnp.clip(1.0 + 0.18 * jax.random.normal(arg_keys[4], (D,), jnp.float32), 0.1, 1.9),
        "retained_lists": draw_retained_lists(jax.random.fold_in(jax.random.fold_in(arg_keys[9], part), 71), part),
        "counts": draw_counts(jax.random.fold_in(jax.random.fold_in(arg_keys[9], part), 71), part),
        "affine_matrix": gaussian(arg_keys[7], (D, QKVW), D ** -0.5, 0.0625, ((0, 8), (1, 2))),
        "affine_offset_vector": gaussian(arg_keys[8], (QKVW,), 0.5, 3.0, ((0, 2),), jnp.float32),
    }


def reference(queries, keys, values, hidden, norm_gain, retained_lists, counts, affine_matrix, affine_offset_vector):
    asker_line_tile = queries.shape[0]
    group_width = QUERY_HEADS // KEY_VALUE_HEADS
    positions = jnp.arange(asker_line_tile, dtype=jnp.int32)
    allowed = positions[None, :] <= positions[:, None]
    query_heads = queries.reshape(asker_line_tile, QUERY_HEADS, HEAD_SIZE).transpose(1, 0, 2)
    key_head_rows = keys.reshape(asker_line_tile, KEY_VALUE_HEADS, HEAD_SIZE).transpose(1, 0, 2)
    value_head_rows = values.reshape(asker_line_tile, KEY_VALUE_HEADS, HEAD_SIZE).transpose(1, 0, 2)

    def one_head(head):
        kv_index = head // group_width
        query_one = lax.dynamic_index_in_dim(query_heads, head, 0, keepdims=False)
        key_one = lax.dynamic_index_in_dim(key_head_rows, kv_index, 0, keepdims=False)
        value_one = lax.dynamic_index_in_dim(value_head_rows, kv_index, 0, keepdims=False)
        scores = jnp.dot(query_one, key_one.T, preferred_element_type=jnp.float32) * HEAD_SIZE ** (-0.5)
        row_max = lax.optimization_barrier(jnp.max(jnp.where(allowed, scores, -1e+30), axis=1))
        weights = jnp.where(allowed, jnp.exp(scores - row_max[:, None]), 0.0)
        row_sum = lax.optimization_barrier(jnp.sum(weights, axis=1))
        mixed = jnp.dot(weights.astype(jnp.bfloat16), value_one, preferred_element_type=jnp.float32) / row_sum[:, None]
        column = lax.optimization_barrier(jnp.sum(weights / row_sum[:, None], axis=0))
        return (mixed, column)
    mixed_all, columns = lax.map(one_head, jnp.arange(QUERY_HEADS, dtype=jnp.int32))
    context = mixed_all.transpose(1, 0, 2).reshape(asker_line_tile, QUERY_HEADS * HEAD_SIZE)
    col_scores = lax.optimization_barrier(jnp.sum(columns, axis=0)) / QUERY_HEADS
    hidden_f = hidden.astype(jnp.float32)
    rescaled_activations = (hidden_f * lax.rsqrt(lax.optimization_barrier(jnp.mean(hidden_f * hidden_f, axis=1, keepdims=True)) + 1e-06) * norm_gain).astype(jnp.bfloat16)
    shard_count = counts.shape[0]
    partition_inner_lines = asker_line_tile // shard_count
    retained_total = asker_line_tile // 2
    retained_element = jnp.arange(retained_total, dtype=jnp.int32)
    partition_finish_marks = jnp.cumsum(counts).astype(jnp.int32)
    holder_partition = lax.optimization_barrier(jnp.sum((partition_finish_marks[None, :] <= retained_element[:, None]).astype(jnp.int32), axis=1))
    starts = partition_finish_marks - counts
    opening_marks = lax.optimization_barrier(jnp.sum(jnp.where(jnp.arange(shard_count, dtype=jnp.int32)[None, :] == holder_partition[:, None], starts[None, :], 0), axis=1))
    retained_place_number = retained_element - opening_marks
    partition_inner_position = retained_lists[holder_partition * partition_inner_lines + retained_place_number]
    retained_elements = rescaled_activations[holder_partition * partition_inner_lines + partition_inner_position]
    tier_third_mapped_triples = jnp.dot(retained_elements, affine_matrix, preferred_element_type=jnp.float32) + affine_offset_vector
    return (context, col_scores, tier_third_mapped_triples)
```

```python
import functools
import math

import jax
import jax.numpy as jnp
from jax import lax
from jax.experimental import pallas as pl
from jax.experimental.pallas import tpu as pltpu
from jax.sharding import PartitionSpec as P

HEAD_SIZE = 128
QUERY_HEADS = 32
F32 = jnp.float32
BF16 = jnp.bfloat16


def remote(src, dst, send_sem, recv_sem, where):
    return pltpu.make_async_remote_copy(
        src_ref=src,
        dst_ref=dst,
        send_sem=send_sem,
        recv_sem=recv_sem,
        device_id=where,
        device_id_type=pl.DeviceIdType.MESH,
    )


def kernel(
    n,
    q_ref, k_ref, v_ref, h_ref, gain_ref, list_ref, count_ref, a_hbm, bias_ref,
    ctx_ref, col_ref, out_ref,
    a_ref, kbuf, vbuf, s_ref, e_ref, sel_send, sel_recv, g_ref, comp_ref,
    y_send, y_recv, own_ref, z_send, z_recv, c_send, c_recv, ct_send, ct_recv,
    a_sem, kv_ssem, kv_rsem, sv_ssem, sv_rsem, fw_ssem, fw_rsem,
    y_ssem, y_rsem, z_ssem, z_rsem, c_ssem, c_rsem, ct_ssem, ct_rsem,
):
    me = lax.axis_index("seq")
    ten = lax.axis_index("ten")
    sibling = {"ten": 1 - ten}
    rows = q_ref.shape[0]
    key_total = n * rows
    kv_heads = k_ref.shape[1] // HEAD_SIZE
    group = q_ref.shape[1] // k_ref.shape[1]
    width = h_ref.shape[1]
    half = width // n // 2
    out_rows = out_ref.shape[0]
    chunk = y_recv.shape[2]
    chunks = y_recv.shape[0]
    pairs = n // 2
    parity = lax.rem(me, 2)
    pair = lax.div(me, 2)
    partner = {"seq": me + 1 - 2 * parity}

    a_copy = pltpu.make_async_copy(a_hbm, a_ref, a_sem)
    a_copy.start()
    kbuf[...] = jnp.zeros_like(kbuf)
    vbuf[...] = jnp.zeros_like(vbuf)
    kbuf[me] = k_ref[...]
    vbuf[me] = v_ref[...]

    barrier = pltpu.get_barrier_semaphore()
    for d in range(1, n):
        pl.semaphore_signal(
            barrier, inc=1, device_id={"seq": lax.rem(me + d, n)},
            device_id_type=pl.DeviceIdType.MESH,
        )
    pl.semaphore_signal(
        barrier, inc=1, device_id=sibling, device_id_type=pl.DeviceIdType.MESH
    )
    pl.semaphore_wait(barrier, n)

    def kv_copies(d, source, target):
        return (
            remote(k_ref, kbuf.at[source], kv_ssem.at[0, d], kv_rsem.at[0, d], {"seq": target}),
            remote(v_ref, vbuf.at[source], kv_ssem.at[1, d], kv_rsem.at[1, d], {"seq": target}),
        )

    for d in range(1, n):

        @pl.when(me + d < n)
        def _():
            for copy in kv_copies(d, me, me + d):
                copy.start()

    square = jnp.zeros((rows, 1), F32)
    step = math.gcd(width, 1024)
    for c in range(width // step):
        x = h_ref[:, c * step:(c + 1) * step].astype(F32)
        square = square + jnp.sum(x * x, axis=1, keepdims=True)
    rescale = lax.rsqrt(square / width + 1e-06)
    lane = lax.broadcasted_iota(jnp.int32, (rows, rows), 1)
    line = lax.broadcasted_iota(jnp.int32, (rows, rows), 0)
    kept = jnp.sum(jnp.where(lane == line, list_ref[...], 0), axis=1, keepdims=True)
    selector = (kept == lane).astype(F32).astype(BF16)

    def chosen(owner):
        columns = pl.ds(pl.multiple_of(owner * (2 * half) + ten * half, 128), half)
        x = h_ref[:, columns].astype(F32) * rescale * gain_ref[:, columns]
        return jnp.dot(selector, x.astype(BF16), preferred_element_type=F32).astype(BF16)

    def sel_copy(d, source, target):
        return remote(
            sel_send.at[d], sel_recv.at[ten, source], sv_ssem.at[d], sv_rsem.at[d], {"seq": target}
        )

    for d in range(1, n):
        owner = lax.rem(me + d, n)
        sel_send[d] = chosen(owner)
        sel_copy(d, me, owner).start()
    sel_recv[ten, me] = chosen(me)

    def forward(d):
        source = lax.rem(me - d + n, n)
        block = sel_recv.at[ten, source]
        return remote(block, block, fw_ssem.at[d], fw_rsem.at[d], sibling)

    forward(0).start()

    at = lax.broadcasted_iota(jnp.int32, (1, key_total), 1)
    place = jnp.full((1, key_total), -1, jnp.int32)
    start = jnp.int32(0)
    for s in range(n):
        t = at - s * rows
        place = jnp.where((t >= 0) & (t < count_ref[s]), start + t, place)
        start = start + count_ref[s]
    row_at = lax.broadcasted_iota(jnp.int32, (out_rows, key_total), 0)
    for side in range(2):
        side_parity = 1 - parity if side == 0 else parity
        for d in range(pairs):
            base = (2 * lax.rem(pair + d, pairs) + side_parity) * out_rows
            first = (side * pairs + d) * out_rows
            g_ref[first:first + out_rows, :] = (
                (row_at + base == place).astype(F32).astype(BF16)
            )

    for d in range(1, n):

        @pl.when(me - d >= 0)
        def _():
            for copy in kv_copies(d, me - d, me):
                copy.wait_recv()

    key_pos = lax.broadcasted_iota(jnp.int32, (rows, key_total), 1)
    query_pos = me * rows + lax.broadcasted_iota(jnp.int32, (rows, key_total), 0)
    allowed = key_pos <= query_pos
    columns_total = jnp.zeros((8, key_total), F32)
    for h in range(kv_heads):
        heads = slice(h * HEAD_SIZE, (h + 1) * HEAD_SIZE)
        query = jnp.concatenate(
            [
                q_ref[:, (h * group + a) * HEAD_SIZE:(h * group + a + 1) * HEAD_SIZE]
                for a in range(group)
            ],
            axis=0,
        )
        key = kbuf[:, :, heads].reshape(key_total, HEAD_SIZE)
        value = vbuf[:, :, heads].reshape(key_total, HEAD_SIZE)
        s_ref[...] = lax.dot_general(
            query, key, (((1,), (1,)), ((), ())), preferred_element_type=F32
        )
        inverses = []
        for a in range(group):
            lines = slice(a * rows, (a + 1) * rows)
            scores = jnp.where(allowed, s_ref[lines, :] * HEAD_SIZE ** (-0.5), -1e30)
            largest = jnp.max(scores, axis=1, keepdims=True)
            weights = jnp.where(allowed, jnp.exp(scores - largest), 0.0)
            e_ref[lines, :] = weights.astype(BF16)
            inverse = 1.0 / jnp.sum(weights, axis=1, keepdims=True)
            inverses.append(inverse)
            columns_total = columns_total + jnp.sum(
                (weights * inverse).reshape(rows // 8, 8, key_total), axis=0
            )
        mixed = jnp.dot(e_ref[...], value, preferred_element_type=F32)
        for a in range(group):
            place_at = (h * group + a) * HEAD_SIZE
            ctx_ref[:, place_at:place_at + HEAD_SIZE] = (
                mixed[a * rows:(a + 1) * rows] * inverses[a]
            )
    lanes = c_send.shape[2]
    per = lanes // rows
    for b in range(n // per):
        c_send[b] = columns_total[:, b * lanes:(b + 1) * lanes]

    def col_copy(d, owner, target):
        return remote(
            c_send.at[lax.div(owner, per)], c_recv.at[d], c_ssem.at[d], c_rsem.at[d],
            {"seq": target},
        )

    for d in range(1, n):

        @pl.when(me - d >= 0)
        def _():
            col_copy(d, me - d, me - d).start()

    for d in range(1, n):
        sel_copy(d, lax.rem(me - d + n, n), me).wait_recv()
        forward(d).start()
    for d in range(n):
        source = lax.rem(me - d + n, n)
        block = sel_recv.at[1 - ten, source]
        remote(block, block, fw_ssem.at[d], fw_rsem.at[d], sibling).wait_recv()
    for side in range(2):
        comp_ref[:, side * half:(side + 1) * half] = jnp.dot(
            g_ref[...], sel_recv[side].reshape(key_total, half), preferred_element_type=F32
        ).astype(BF16)
    a_copy.wait()

    side_rows = pairs * out_rows

    def y_copy(c):
        return remote(y_send.at[c], y_recv.at[c], y_ssem.at[c], y_rsem.at[c], partner)

    def z_copy(c, d):
        target = {"seq": 2 * lax.rem(pair + d, pairs) + parity}
        return remote(
            z_send.at[c, d], z_recv.at[c, d], z_ssem.at[c, d], z_rsem.at[c, d], target
        )

    def pass_on(c):
        y_copy(c).wait_recv()
        for d in range(1, pairs):
            part = slice(d * out_rows, (d + 1) * out_rows)
            z_send[c, d] = (own_ref[c, part, :] + y_recv[c, part, :].astype(F32)).astype(BF16)
            z_copy(c, d).start()

    for c in range(chunks):
        columns = slice(c * chunk, (c + 1) * chunk)
        y_send[c] = jnp.dot(
            comp_ref[:side_rows, :], a_ref[:, columns], preferred_element_type=F32
        ).astype(BF16)
        y_copy(c).start()
        own_ref[c] = jnp.dot(
            comp_ref[side_rows:, :], a_ref[:, columns], preferred_element_type=F32
        )
        if c > 0:
            pass_on(c - 1)
    pass_on(chunks - 1)

    zero = jnp.int32(0)
    mine = c_send[lax.div(me, per)]
    for d in range(1, n):
        c_recv_valid = me + d < n

        @pl.when(c_recv_valid)
        def _():
            col_copy(d, me, me).wait_recv()

        @pl.when(jnp.logical_not(c_recv_valid))
        def _():
            c_recv[d] = jnp.zeros_like(c_recv[d])

        mine = mine + c_recv[d]
    ct_send[...] = mine
    ct = remote(ct_send, ct_recv, ct_ssem, ct_rsem, sibling)
    ct.start()

    for c in range(chunks):
        columns = slice(c * chunk, (c + 1) * chunk)
        total = own_ref[c, :out_rows, :] + y_recv[c, :out_rows, :].astype(F32)
        for d in range(1, pairs):
            z_copy(c, d).wait_recv()
            total = total + z_recv[c, d].astype(F32)
        out_ref[:, columns] = total + bias_ref[:, columns]

    ct.wait()
    both = jnp.sum(ct_send[...] + ct_recv[...], axis=0, keepdims=True) / QUERY_HEADS
    turn = lax.rem(me, per)
    picked = both[:, :rows]
    for b in range(1, per):
        picked = jnp.where(turn == b, both[:, b * rows:(b + 1) * rows], picked)
    col_ref[...] = picked

    for d in range(1, n):

        @pl.when(me + d < n)
        def _():
            for copy in kv_copies(d, me, me + d):
                copy.wait_send()

        @pl.when(me - d >= 0)
        def _():
            col_copy(d, me - d, me - d).wait_send()

        sel_copy(d, me, lax.rem(me + d, n)).wait_send()
    for d in range(n):
        forward(d).wait_send()
    for c in range(chunks):
        y_copy(c).wait_send()
        for d in range(1, pairs):
            z_copy(c, d).wait_send()


def shards(
    n, queries, keys, values, hidden, norm_gain, retained_lists, counts, affine_matrix,
    affine_offset_vector,
):
    rows, query_width = queries.shape
    width = hidden.shape[1]
    depth, columns = affine_matrix.shape
    kv_width = keys.shape[1]
    group = query_width // kv_width
    half = width // n // 2
    out_rows = rows // 2
    kept_total = n * out_rows
    chunk = math.gcd(columns, 512)
    chunks = columns // chunk
    pairs = n // 2
    lanes = max(128, rows)
    key_total = n * rows
    vmem = pl.BlockSpec(memory_space=pltpu.VMEM)
    dma = pltpu.SemaphoreType.DMA
    context, col_scores, projected = pl.pallas_call(
        functools.partial(kernel, n),
        out_shape=(
            jax.ShapeDtypeStruct((rows, query_width), F32),
            jax.ShapeDtypeStruct((1, rows), F32),
            jax.ShapeDtypeStruct((out_rows, columns), F32),
        ),
        in_specs=[
            vmem, vmem, vmem, vmem, vmem, vmem,
            pl.BlockSpec(memory_space=pltpu.SMEM),
            pl.BlockSpec(memory_space=pl.ANY),
            vmem,
        ],
        out_specs=(vmem, vmem, vmem),
        scratch_shapes=[
            pltpu.VMEM((depth, columns), BF16),
            pltpu.VMEM((n, rows, kv_width), BF16),
            pltpu.VMEM((n, rows, kv_width), BF16),
            pltpu.VMEM((group * rows, key_total), F32),
            pltpu.VMEM((group * rows, key_total), BF16),
            pltpu.VMEM((n, rows, half), BF16),
            pltpu.VMEM((2, n, rows, half), BF16),
            pltpu.VMEM((kept_total, key_total), BF16),
            pltpu.VMEM((kept_total, 2 * half), BF16),
            pltpu.VMEM((chunks, kept_total // 2, chunk), BF16),
            pltpu.VMEM((chunks, kept_total // 2, chunk), BF16),
            pltpu.VMEM((chunks, kept_total // 2, chunk), F32),
            pltpu.VMEM((chunks, pairs, out_rows, chunk), BF16),
            pltpu.VMEM((chunks, pairs, out_rows, chunk), BF16),
            pltpu.VMEM((key_total // lanes, 8, lanes), F32),
            pltpu.VMEM((n, 8, lanes), F32),
            pltpu.VMEM((8, lanes), F32),
            pltpu.VMEM((8, lanes), F32),
            dma,
            dma((2, n)), dma((2, n)),
            dma((n,)), dma((n,)),
            dma((n,)), dma((n,)),
            dma((chunks,)), dma((chunks,)),
            dma((chunks, pairs)), dma((chunks, pairs)),
            dma((n,)), dma((n,)),
            dma, dma,
        ],
        compiler_params=pltpu.CompilerParams(collective_id=0, has_side_effects=True),
    )(
        queries, keys, values, hidden, norm_gain.reshape(1, width),
        retained_lists.reshape(1, rows), counts, affine_matrix,
        affine_offset_vector.reshape(1, columns),
    )
    return (context, col_scores.reshape(rows), projected)


def solution(mesh):
    in_specs = (
        P(("grp", "seq"), "ten"),
        P(("grp", "seq"), "ten"),
        P(("grp", "seq"), "ten"),
        P(("grp", "seq"), None),
        P(),
        P(("grp", "seq")),
        P("grp"),
        P("seq", "ten"),
        P("ten"),
    )
    out_specs = (P(("grp", "seq"), "ten"), P(("grp", "seq")), P(("grp", "seq"), "ten"))
    return jax.shard_map(
        functools.partial(shards, mesh.shape["seq"]),
        mesh=mesh, in_specs=in_specs, out_specs=out_specs, check_vma=False,
    )
```

```python
import functools
import math

import jax
import jax.numpy as jnp
from jax import lax
from jax.experimental import pallas as pl
from jax.experimental.pallas import tpu as pltpu
from jax.sharding import PartitionSpec as P

HEAD_SIZE = 128
QUERY_HEADS = 32
F32 = jnp.float32
BF16 = jnp.bfloat16


def remote(src, dst, send_sem, recv_sem, where):
    return pltpu.make_async_remote_copy(
        src_ref=src,
        dst_ref=dst,
        send_sem=send_sem,
        recv_sem=recv_sem,
        device_id=where,
        device_id_type=pl.DeviceIdType.MESH,
    )


def kernel(
    n,
    q_ref, k_ref, v_ref, h_ref, gain_ref, list_ref, count_ref, a_hbm, bias_ref,
    ctx_ref, col_ref, out_ref,
    a_ref, kvbuf, s_ref, e_ref, sel_send, sel_recv, g_ref, comp_ref,
    y_send, y_recv, own_ref, x_send, x_recv, z_send, z_recv, c_send, c_recv, ct_send, ct_recv,
    a_sem, kz_ssem, kz_rsem, ky_ssem, ky_rsem, sv_ssem, sv_rsem, fw_ssem, fw_rsem,
    y_ssem, y_rsem, x_ssem, x_rsem, z_ssem, z_rsem, c_ssem, c_rsem, ct_ssem, ct_rsem,
):
    me = lax.axis_index("seq")
    ten = lax.axis_index("ten")
    sibling = {"ten": 1 - ten}
    rows = q_ref.shape[0]
    key_total = n * rows
    kv_heads = k_ref.shape[1] // HEAD_SIZE
    group = q_ref.shape[1] // k_ref.shape[1]
    width = h_ref.shape[1]
    half = width // n // 2
    out_rows = out_ref.shape[0]
    chunk = y_recv.shape[2]
    chunks = y_recv.shape[0]
    pairs = n // 2
    parity = lax.rem(me, 2)
    pair = lax.div(me, 2)
    partner = {"seq": me + 1 - 2 * parity}
    quads = pairs // 2
    pair_parity = lax.rem(pair, 2)
    other_pair = pair + 1 - 2 * pair_parity

    a_copy = pltpu.make_async_copy(a_hbm, a_ref, a_sem)
    a_copy.start()
    kvbuf[...] = jnp.zeros_like(kvbuf)
    kvbuf[me, 0] = k_ref[...]
    kvbuf[me, 1] = v_ref[...]

    barrier = pltpu.get_barrier_semaphore()
    for d in range(1, n):
        pl.semaphore_signal(
            barrier, inc=1, device_id={"seq": lax.rem(me + d, n)},
            device_id_type=pl.DeviceIdType.MESH,
        )
    pl.semaphore_signal(
        barrier, inc=1, device_id=sibling, device_id_type=pl.DeviceIdType.MESH
    )
    pl.semaphore_wait(barrier, n)

    def chain(age):
        block = kvbuf.at[2 * (pair - age) + parity]
        target = {"seq": me + 2}
        return remote(block, block, kz_ssem.at[age], kz_rsem.at[age + 1], target)

    def chain_in(age):
        block = kvbuf.at[2 * (pair - age) + parity]
        return remote(block, block, kz_ssem.at[age - 1], kz_rsem.at[age], partner)

    def across(age):
        block = kvbuf.at[2 * (pair - age) + parity]
        return remote(block, block, ky_ssem.at[age], ky_rsem.at[age], partner)

    def across_in(age):
        block = kvbuf.at[2 * (pair - age) + 1 - parity]
        return remote(block, block, ky_ssem.at[age], ky_rsem.at[age], partner)

    @pl.when(pair + 1 < pairs)
    def _():
        chain(0).start()

    @pl.when(parity == 0)
    def _():
        across(0).start()

    def relay(age):
        @pl.when(pair >= age)
        def _():
            chain_in(age).wait_recv()
            across(age).start()

        if age + 1 < pairs:

            @pl.when((pair >= age) & (pair + 1 < pairs))
            def _():
                chain(age).start()

    square = jnp.zeros((rows, 1), F32)
    step = math.gcd(width, 1024)
    for c in range(width // step):
        x = h_ref[:, c * step:(c + 1) * step].astype(F32)
        square = square + jnp.sum(x * x, axis=1, keepdims=True)
    rescale = lax.rsqrt(square / width + 1e-06)
    lane = lax.broadcasted_iota(jnp.int32, (rows, rows), 1)
    line = lax.broadcasted_iota(jnp.int32, (rows, rows), 0)
    kept = jnp.sum(jnp.where(lane == line, list_ref[...], 0), axis=1, keepdims=True)
    selector = (kept == lane).astype(F32).astype(BF16)

    def chosen(owner):
        columns = pl.ds(pl.multiple_of(owner * (2 * half) + ten * half, 128), half)
        x = h_ref[:, columns].astype(F32) * rescale * gain_ref[:, columns]
        return jnp.dot(selector, x.astype(BF16), preferred_element_type=F32).astype(BF16)

    def sel_copy(d, source, target):
        return remote(
            sel_send.at[d], sel_recv.at[ten, source], sv_ssem.at[d], sv_rsem.at[d], {"seq": target}
        )

    order = sorted(range(1, n), key=lambda d: abs(2 * d - n))
    for at, d in enumerate(order):
        owner = lax.rem(me + d, n)
        sel_send[d] = chosen(owner)
        sel_copy(d, me, owner).start()
        if at % 2 == 1 and at // 2 + 1 < pairs:
            relay(at // 2 + 1)
    sel_recv[ten, me] = chosen(me)

    def forward(d):
        source = lax.rem(me - d + n, n)
        block = sel_recv.at[ten, source]
        return remote(block, block, fw_ssem.at[d], fw_rsem.at[d], sibling)

    forward(0).start()

    at = lax.broadcasted_iota(jnp.int32, (1, key_total), 1)
    place = jnp.full((1, key_total), -1, jnp.int32)
    start = jnp.int32(0)
    for s in range(n):
        t = at - s * rows
        place = jnp.where((t >= 0) & (t < count_ref[s]), start + t, place)
        start = start + count_ref[s]
    row_at = lax.broadcasted_iota(jnp.int32, (out_rows, key_total), 0)
    for side in range(2):
        side_parity = 1 - parity if side == 0 else parity
        for d in range(pairs):
            origin = other_pair if d < quads else pair
            base = (2 * lax.rem(origin + 2 * (d % quads), pairs) + side_parity) * out_rows
            first = (side * pairs + d) * out_rows
            g_ref[first:first + out_rows, :] = (
                (row_at + base == place).astype(F32).astype(BF16)
            )

    @pl.when(parity == 1)
    def _():
        across_in(0).wait_recv()

    for age in range(1, pairs):

        @pl.when(pair >= age)
        def _():
            across_in(age).wait_recv()

    key_pos = lax.broadcasted_iota(jnp.int32, (rows, key_total), 1)
    query_pos = me * rows + lax.broadcasted_iota(jnp.int32, (rows, key_total), 0)
    allowed = key_pos <= query_pos
    columns_total = jnp.zeros((8, key_total), F32)
    for h in range(kv_heads):
        heads = slice(h * HEAD_SIZE, (h + 1) * HEAD_SIZE)
        query = jnp.concatenate(
            [
                q_ref[:, (h * group + a) * HEAD_SIZE:(h * group + a + 1) * HEAD_SIZE]
                for a in range(group)
            ],
            axis=0,
        )
        key = kvbuf[:, 0, :, heads].reshape(key_total, HEAD_SIZE)
        value = kvbuf[:, 1, :, heads].reshape(key_total, HEAD_SIZE)
        s_ref[...] = lax.dot_general(
            query, key, (((1,), (1,)), ((), ())), preferred_element_type=F32
        )
        inverses = []
        for a in range(group):
            lines = slice(a * rows, (a + 1) * rows)
            scores = jnp.where(allowed, s_ref[lines, :] * HEAD_SIZE ** (-0.5), -1e30)
            largest = jnp.max(scores, axis=1, keepdims=True)
            weights = jnp.where(allowed, jnp.exp(scores - largest), 0.0)
            e_ref[lines, :] = weights.astype(BF16)
            inverse = 1.0 / jnp.sum(weights, axis=1, keepdims=True)
            inverses.append(inverse)
            columns_total = columns_total + jnp.sum(
                (weights * inverse).reshape(rows // 8, 8, key_total), axis=0
            )
        mixed = jnp.dot(e_ref[...], value, preferred_element_type=F32)
        for a in range(group):
            place_at = (h * group + a) * HEAD_SIZE
            ctx_ref[:, place_at:place_at + HEAD_SIZE] = (
                mixed[a * rows:(a + 1) * rows] * inverses[a]
            )
    lanes = c_send.shape[2]
    per = lanes // rows
    for b in range(n // per):
        c_send[b] = columns_total[:, b * lanes:(b + 1) * lanes]

    def col_copy(d, owner, target):
        return remote(
            c_send.at[lax.div(owner, per)], c_recv.at[d], c_ssem.at[d], c_rsem.at[d],
            {"seq": target},
        )

    for d in range(1, n):

        @pl.when(me - d >= 0)
        def _():
            col_copy(d, me - d, me - d).start()

    for d in order:
        sel_copy(d, lax.rem(me - d + n, n), me).wait_recv()
        forward(d).start()
    for d in range(n):
        source = lax.rem(me - d + n, n)
        block = sel_recv.at[1 - ten, source]
        remote(block, block, fw_ssem.at[d], fw_rsem.at[d], sibling).wait_recv()
    for side in range(2):
        comp_ref[:, side * half:(side + 1) * half] = jnp.dot(
            g_ref[...], sel_recv[side].reshape(key_total, half), preferred_element_type=F32
        ).astype(BF16)
    a_copy.wait()

    side_rows = pairs * out_rows

    def y_copy(c):
        return remote(y_send.at[c], y_recv.at[c], y_ssem.at[c], y_rsem.at[c], partner)

    def x_copy(c):
        target = {"seq": 2 * other_pair + parity}
        return remote(x_send.at[c], x_recv.at[c], x_ssem.at[c], x_rsem.at[c], target)

    def z_copy(c, d):
        target = {"seq": 2 * lax.rem(pair + 2 * d, pairs) + parity}
        return remote(
            z_send.at[c, d], z_recv.at[c, d], z_ssem.at[c, d], z_rsem.at[c, d], target
        )

    quad_rows = quads * out_rows

    def to_other_pair(c):
        y_copy(c).wait_recv()
        x_send[c] = (
            own_ref[c, :quad_rows, :] + y_recv[c, :quad_rows, :].astype(F32)
        ).astype(BF16)
        x_copy(c).start()

    def to_owners(c):
        x_copy(c).wait_recv()
        for d in range(quads):
            part = slice(quad_rows + d * out_rows, quad_rows + (d + 1) * out_rows)
            total = (
                own_ref[c, part, :]
                + y_recv[c, part, :].astype(F32)
                + x_recv[c, d * out_rows:(d + 1) * out_rows, :].astype(F32)
            )
            if d == 0:
                own_ref[c, part, :] = total
            else:
                z_send[c, d] = total.astype(BF16)
                z_copy(c, d).start()

    for c in range(chunks):
        columns = slice(c * chunk, (c + 1) * chunk)
        y_send[c] = jnp.dot(
            comp_ref[:side_rows, :], a_ref[:, columns], preferred_element_type=F32
        ).astype(BF16)
        y_copy(c).start()
        own_ref[c] = jnp.dot(
            comp_ref[side_rows:, :], a_ref[:, columns], preferred_element_type=F32
        )
    for c in range(chunks):
        to_other_pair(c)
        if c > 0:
            to_owners(c - 1)
    to_owners(chunks - 1)

    mine = c_send[lax.div(me, per)]
    for d in range(1, n):
        c_recv_valid = me + d < n

        @pl.when(c_recv_valid)
        def _():
            col_copy(d, me, me).wait_recv()

        @pl.when(jnp.logical_not(c_recv_valid))
        def _():
            c_recv[d] = jnp.zeros_like(c_recv[d])

        mine = mine + c_recv[d]
    ct_send[...] = mine
    ct = remote(ct_send, ct_recv, ct_ssem, ct_rsem, sibling)
    ct.start()

    for c in range(chunks):
        columns = slice(c * chunk, (c + 1) * chunk)
        total = own_ref[c, quad_rows:quad_rows + out_rows, :]
        for d in range(1, quads):
            z_copy(c, d).wait_recv()
            total = total + z_recv[c, d].astype(F32)
        out_ref[:, columns] = total + bias_ref[columns].reshape(1, chunk)

    ct.wait()
    both = jnp.sum(ct_send[...] + ct_recv[...], axis=0, keepdims=True) / QUERY_HEADS
    turn = lax.rem(me, per)
    picked = both[:, :rows]
    for b in range(1, per):
        picked = jnp.where(turn == b, both[:, b * rows:(b + 1) * rows], picked)
    col_ref[...] = picked

    for d in range(1, n):

        @pl.when(me - d >= 0)
        def _():
            col_copy(d, me - d, me - d).wait_send()

        sel_copy(d, me, lax.rem(me + d, n)).wait_send()
    @pl.when(parity == 0)
    def _():
        across(0).wait_send()

    @pl.when(pair + 1 < pairs)
    def _():
        chain(0).wait_send()

    for age in range(1, pairs):

        @pl.when(pair >= age)
        def _():
            across(age).wait_send()

        if age + 1 < pairs:

            @pl.when((pair >= age) & (pair + 1 < pairs))
            def _():
                chain(age).wait_send()

    for d in range(n):
        forward(d).wait_send()
    for c in range(chunks):
        y_copy(c).wait_send()
        x_copy(c).wait_send()
        for d in range(1, quads):
            z_copy(c, d).wait_send()


def hand_over(context, scores, projected, context_out, scores_out, projected_out):
    context_out[...] = context[...]
    scores_out[...] = scores[...]
    projected_out[...] = projected[...]


def shards(
    n, queries, keys, values, hidden, norm_gain, retained_lists, counts, affine_matrix,
    affine_offset_vector,
):
    rows, query_width = queries.shape
    width = hidden.shape[1]
    depth, columns = affine_matrix.shape
    kv_width = keys.shape[1]
    group = query_width // kv_width
    half = width // n // 2
    out_rows = rows // 2
    kept_total = n * out_rows
    chunk = math.gcd(columns, 512)
    chunks = columns // chunk
    pairs = n // 2
    quads = n // 4
    lanes = max(128, rows)
    key_total = n * rows
    vmem = pl.BlockSpec(memory_space=pltpu.VMEM)
    dma = pltpu.SemaphoreType.DMA
    context, col_scores, projected = pl.pallas_call(
        functools.partial(kernel, n),
        out_shape=(
            jax.ShapeDtypeStruct((rows, query_width), F32),
            jax.ShapeDtypeStruct((1, rows), F32),
            jax.ShapeDtypeStruct((out_rows, columns), F32),
        ),
        in_specs=[
            vmem, vmem, vmem, vmem, vmem, vmem,
            pl.BlockSpec(memory_space=pltpu.SMEM),
            pl.BlockSpec(memory_space=pl.ANY),
            vmem,
        ],
        out_specs=(vmem, vmem, vmem),
        scratch_shapes=[
            pltpu.VMEM((depth, columns), BF16),
            pltpu.VMEM((n, 2, rows, kv_width), BF16),
            pltpu.VMEM((group * rows, key_total), F32),
            pltpu.VMEM((group * rows, key_total), BF16),
            pltpu.VMEM((n, rows, half), BF16),
            pltpu.VMEM((2, n, rows, half), BF16),
            pltpu.VMEM((kept_total, key_total), BF16),
            pltpu.VMEM((kept_total, 2 * half), BF16),
            pltpu.VMEM((chunks, kept_total // 2, chunk), BF16),
            pltpu.VMEM((chunks, kept_total // 2, chunk), BF16),
            pltpu.VMEM((chunks, kept_total // 2, chunk), F32),
            pltpu.VMEM((chunks, kept_total // 4, chunk), BF16),
            pltpu.VMEM((chunks, kept_total // 4, chunk), BF16),
            pltpu.VMEM((chunks, quads, out_rows, chunk), BF16),
            pltpu.VMEM((chunks, quads, out_rows, chunk), BF16),
            pltpu.VMEM((key_total // lanes, 8, lanes), F32),
            pltpu.VMEM((n, 8, lanes), F32),
            pltpu.VMEM((8, lanes), F32),
            pltpu.VMEM((8, lanes), F32),
            dma,
            dma((pairs,)), dma((pairs,)),
            dma((pairs,)), dma((pairs,)),
            dma((n,)), dma((n,)),
            dma((n,)), dma((n,)),
            dma((chunks,)), dma((chunks,)),
            dma((chunks,)), dma((chunks,)),
            dma((chunks, quads)), dma((chunks, quads)),
            dma((n,)), dma((n,)),
            dma, dma,
        ],
        compiler_params=pltpu.CompilerParams(collective_id=0, has_side_effects=True),
    )(
        queries, keys, values, hidden, norm_gain.reshape(1, width),
        retained_lists.reshape(1, rows), counts, affine_matrix,
        affine_offset_vector,
    )
    context, col_scores, projected = pl.pallas_call(
        hand_over,
        out_shape=(
            jax.ShapeDtypeStruct(context.shape, F32),
            jax.ShapeDtypeStruct(col_scores.shape, F32),
            jax.ShapeDtypeStruct(projected.shape, F32),
        ),
        in_specs=[vmem, vmem, vmem],
        out_specs=(vmem, vmem, vmem),
    )(context, col_scores, projected)
    return (context, col_scores.reshape(rows), projected)


def solution(mesh):
    in_specs = (
        P(("grp", "seq"), "ten"),
        P(("grp", "seq"), "ten"),
        P(("grp", "seq"), "ten"),
        P(("grp", "seq"), None),
        P(),
        P(("grp", "seq")),
        P("grp"),
        P("seq", "ten"),
        P("ten"),
    )
    out_specs = (P(("grp", "seq"), "ten"), P(("grp", "seq")), P(("grp", "seq"), "ten"))
    return jax.shard_map(
        functools.partial(shards, mesh.shape["seq"]),
        mesh=mesh, in_specs=in_specs, out_specs=out_specs, check_vma=False,
    )
```

```python
import functools
import math

import jax
import jax.numpy as jnp
from jax import lax
from jax.experimental import pallas as pl
from jax.experimental.pallas import tpu as pltpu
from jax.sharding import PartitionSpec as P

HEAD_SIZE = 128
QUERY_HEADS = 32
F32 = jnp.float32
BF16 = jnp.bfloat16


def remote(src, dst, send_sem, recv_sem, where):
    return pltpu.make_async_remote_copy(
        src_ref=src,
        dst_ref=dst,
        send_sem=send_sem,
        recv_sem=recv_sem,
        device_id=where,
        device_id_type=pl.DeviceIdType.MESH,
    )


def kernel(
    n,
    q_ref, k_ref, v_ref, h_ref, gain_ref, list_ref, count_ref, a_hbm, bias_ref,
    ctx_ref, col_ref, out_ref,
    a_ref, kvbuf, s_ref, e_ref, sel_send, sel_recv, g_ref, comp_ref,
    y_send, y_recv, own_ref, x_send, x_recv, z_send, z_recv, c_send, c_recv, ct_send, ct_recv,
    a_sem, kz_ssem, kz_rsem, ky_ssem, ky_rsem, sv_ssem, sv_rsem, fw_ssem, fw_rsem,
    y_ssem, y_rsem, x_ssem, x_rsem, z_ssem, z_rsem, c_ssem, c_rsem, ct_ssem, ct_rsem,
):
    me = lax.axis_index("seq")
    ten = lax.axis_index("ten")
    sibling = {"ten": 1 - ten}
    rows = q_ref.shape[0]
    key_total = n * rows
    kv_heads = k_ref.shape[1] // HEAD_SIZE
    group = q_ref.shape[1] // k_ref.shape[1]
    width = h_ref.shape[1]
    half = width // n // 2
    out_rows = out_ref.shape[0]
    chunk = y_recv.shape[2]
    chunks = y_recv.shape[0]
    pairs = n // 2
    parity = lax.rem(me, 2)
    pair = lax.div(me, 2)
    partner = {"seq": me + 1 - 2 * parity}
    quads = pairs // 2
    pair_parity = lax.rem(pair, 2)
    other_pair = pair + 1 - 2 * pair_parity

    a_copy = pltpu.make_async_copy(a_hbm, a_ref, a_sem)
    a_copy.start()
    kvbuf[...] = jnp.zeros_like(kvbuf)
    kvbuf[me, 0] = k_ref[...]
    kvbuf[me, 1] = v_ref[...]

    barrier = pltpu.get_barrier_semaphore()
    for d in range(1, n):
        pl.semaphore_signal(
            barrier, inc=1, device_id={"seq": lax.rem(me + d, n)},
            device_id_type=pl.DeviceIdType.MESH,
        )
    pl.semaphore_signal(
        barrier, inc=1, device_id=sibling, device_id_type=pl.DeviceIdType.MESH
    )
    pl.semaphore_wait(barrier, n)

    def chain(age):
        block = kvbuf.at[2 * (pair - age) + parity]
        target = {"seq": me + 2}
        return remote(block, block, kz_ssem.at[age], kz_rsem.at[age + 1], target)

    def chain_in(age):
        block = kvbuf.at[2 * (pair - age) + parity]
        return remote(block, block, kz_ssem.at[age - 1], kz_rsem.at[age], partner)

    def across(age):
        block = kvbuf.at[2 * (pair - age) + parity]
        return remote(block, block, ky_ssem.at[age], ky_rsem.at[age], partner)

    def across_in(age):
        block = kvbuf.at[2 * (pair - age) + 1 - parity]
        return remote(block, block, ky_ssem.at[age], ky_rsem.at[age], partner)

    @pl.when(pair + 1 < pairs)
    def _():
        chain(0).start()

    @pl.when(parity == 0)
    def _():
        across(0).start()

    def relay(age):
        @pl.when(pair >= age)
        def _():
            chain_in(age).wait_recv()
            across(age).start()

        if age + 1 < pairs:

            @pl.when((pair >= age) & (pair + 1 < pairs))
            def _():
                chain(age).start()

    square = jnp.zeros((rows, 1), F32)
    step = math.gcd(width, 1024)
    for c in range(width // step):
        x = h_ref[:, c * step:(c + 1) * step].astype(F32)
        square = square + jnp.sum(x * x, axis=1, keepdims=True)
    rescale = lax.rsqrt(square / width + 1e-06)
    lane = lax.broadcasted_iota(jnp.int32, (rows, rows), 1)
    line = lax.broadcasted_iota(jnp.int32, (rows, rows), 0)
    kept = jnp.sum(jnp.where(lane == line, list_ref[...], 0), axis=1, keepdims=True)
    selector = (kept == lane).astype(F32).astype(BF16)

    def chosen(owner):
        columns = pl.ds(pl.multiple_of(owner * (2 * half) + ten * half, 128), half)
        x = h_ref[:, columns].astype(F32) * rescale * gain_ref[:, columns]
        return jnp.dot(selector, x.astype(BF16), preferred_element_type=F32).astype(BF16)

    def sel_copy(d, source, target):
        return remote(
            sel_send.at[d], sel_recv.at[ten, source], sv_ssem.at[d], sv_rsem.at[d], {"seq": target}
        )

    order = sorted(range(1, n), key=lambda d: abs(2 * d - n))
    for d in order:
        owner = lax.rem(me + d, n)
        sel_send[d] = chosen(owner)
        sel_copy(d, me, owner).start()
    sel_recv[ten, me] = chosen(me)

    def forward(d):
        source = lax.rem(me - d + n, n)
        block = sel_recv.at[ten, source]
        return remote(block, block, fw_ssem.at[d], fw_rsem.at[d], sibling)

    forward(0).start()

    at = lax.broadcasted_iota(jnp.int32, (1, key_total), 1)
    place = jnp.full((1, key_total), -1, jnp.int32)
    start = jnp.int32(0)
    for s in range(n):
        t = at - s * rows
        place = jnp.where((t >= 0) & (t < count_ref[s]), start + t, place)
        start = start + count_ref[s]
    row_at = lax.broadcasted_iota(jnp.int32, (out_rows, key_total), 0)
    for side in range(2):
        side_parity = 1 - parity if side == 0 else parity
        for d in range(pairs):
            origin = other_pair if d < quads else pair
            base = (2 * lax.rem(origin + 2 * (d % quads), pairs) + side_parity) * out_rows
            first = (side * pairs + d) * out_rows
            g_ref[first:first + out_rows, :] = (
                (row_at + base == place).astype(F32).astype(BF16)
            )

    relay(1)
    for at, d in enumerate(order):
        sel_copy(d, lax.rem(me - d + n, n), me).wait_recv()
        forward(d).start()
        if at % 2 == 0 and 0 < at < n - 2:
            relay(at // 2 + 1)
    for d in range(n):
        source = lax.rem(me - d + n, n)
        block = sel_recv.at[1 - ten, source]
        remote(block, block, fw_ssem.at[d], fw_rsem.at[d], sibling).wait_recv()
    for side in range(2):
        comp_ref[:, side * half:(side + 1) * half] = jnp.dot(
            g_ref[...], sel_recv[side].reshape(key_total, half), preferred_element_type=F32
        ).astype(BF16)
    a_copy.wait()

    side_rows = pairs * out_rows

    def y_copy(c):
        return remote(y_send.at[c], y_recv.at[c], y_ssem.at[c], y_rsem.at[c], partner)

    def x_copy(c):
        target = {"seq": 2 * other_pair + parity}
        return remote(x_send.at[c], x_recv.at[c], x_ssem.at[c], x_rsem.at[c], target)

    def z_copy(c, d):
        target = {"seq": 2 * lax.rem(pair + 2 * d, pairs) + parity}
        return remote(
            z_send.at[c, d], z_recv.at[c, d], z_ssem.at[c, d], z_rsem.at[c, d], target
        )

    quad_rows = quads * out_rows

    def to_other_pair(c):
        y_copy(c).wait_recv()
        x_send[c] = (
            own_ref[c, :quad_rows, :] + y_recv[c, :quad_rows, :].astype(F32)
        ).astype(BF16)
        x_copy(c).start()

    def to_owners(c):
        x_copy(c).wait_recv()
        for d in range(quads):
            part = slice(quad_rows + d * out_rows, quad_rows + (d + 1) * out_rows)
            total = (
                own_ref[c, part, :]
                + y_recv[c, part, :].astype(F32)
                + x_recv[c, d * out_rows:(d + 1) * out_rows, :].astype(F32)
            )
            if d == 0:
                own_ref[c, part, :] = total
            else:
                z_send[c, d] = total.astype(BF16)
                z_copy(c, d).start()

    for c in range(chunks):
        columns = slice(c * chunk, (c + 1) * chunk)
        part = jnp.dot(comp_ref[...], a_ref[:, columns], preferred_element_type=F32)
        y_send[c] = part[:side_rows].astype(BF16)
        y_copy(c).start()
        own_ref[c] = part[side_rows:]

    @pl.when(parity == 1)
    def _():
        across_in(0).wait_recv()

    for age in range(1, pairs):

        @pl.when(pair >= age)
        def _():
            across_in(age).wait_recv()

    key_pos = lax.broadcasted_iota(jnp.int32, (rows, key_total), 1)
    query_pos = me * rows + lax.broadcasted_iota(jnp.int32, (rows, key_total), 0)
    allowed = key_pos <= query_pos
    columns_total = jnp.zeros((8, key_total), F32)
    for h in range(kv_heads):
        heads = slice(h * HEAD_SIZE, (h + 1) * HEAD_SIZE)
        query = jnp.concatenate(
            [
                q_ref[:, (h * group + a) * HEAD_SIZE:(h * group + a + 1) * HEAD_SIZE]
                for a in range(group)
            ],
            axis=0,
        )
        key = kvbuf[:, 0, :, heads].reshape(key_total, HEAD_SIZE)
        value = kvbuf[:, 1, :, heads].reshape(key_total, HEAD_SIZE)
        s_ref[...] = lax.dot_general(
            query, key, (((1,), (1,)), ((), ())), preferred_element_type=F32
        )
        inverses = []
        for a in range(group):
            lines = slice(a * rows, (a + 1) * rows)
            scores = jnp.where(allowed, s_ref[lines, :] * HEAD_SIZE ** (-0.5), -1e30)
            largest = jnp.max(scores, axis=1, keepdims=True)
            weights = jnp.where(allowed, jnp.exp(scores - largest), 0.0)
            e_ref[lines, :] = weights.astype(BF16)
            inverse = 1.0 / jnp.sum(weights, axis=1, keepdims=True)
            inverses.append(inverse)
            columns_total = columns_total + jnp.sum(
                (weights * inverse).reshape(rows // 8, 8, key_total), axis=0
            )
        mixed = jnp.dot(e_ref[...], value, preferred_element_type=F32)
        for a in range(group):
            place_at = (h * group + a) * HEAD_SIZE
            ctx_ref[:, place_at:place_at + HEAD_SIZE] = (
                mixed[a * rows:(a + 1) * rows] * inverses[a]
            )
    lanes = c_send.shape[2]
    per = lanes // rows
    for b in range(n // per):
        c_send[b] = columns_total[:, b * lanes:(b + 1) * lanes]

    def col_copy(d, owner, target):
        return remote(
            c_send.at[lax.div(owner, per)], c_recv.at[d], c_ssem.at[d], c_rsem.at[d],
            {"seq": target},
        )

    for d in range(1, n):

        @pl.when(me - d >= 0)
        def _():
            col_copy(d, me - d, me - d).start()

    for c in range(chunks):
        to_other_pair(c)
        if c > 0:
            to_owners(c - 1)
    to_owners(chunks - 1)

    mine = c_send[lax.div(me, per)]
    for d in range(1, n):
        c_recv_valid = me + d < n

        @pl.when(c_recv_valid)
        def _():
            col_copy(d, me, me).wait_recv()

        @pl.when(jnp.logical_not(c_recv_valid))
        def _():
            c_recv[d] = jnp.zeros_like(c_recv[d])

        mine = mine + c_recv[d]
    ct_send[...] = mine
    ct = remote(ct_send, ct_recv, ct_ssem, ct_rsem, sibling)
    ct.start()

    for c in range(chunks):
        columns = slice(c * chunk, (c + 1) * chunk)
        total = own_ref[c, quad_rows:quad_rows + out_rows, :]
        for d in range(1, quads):
            z_copy(c, d).wait_recv()
            total = total + z_recv[c, d].astype(F32)
        out_ref[:, columns] = total + bias_ref[columns].reshape(1, chunk)

    ct.wait()
    both = jnp.sum(ct_send[...] + ct_recv[...], axis=0, keepdims=True) / QUERY_HEADS
    turn = lax.rem(me, per)
    picked = both[:, :rows]
    for b in range(1, per):
        picked = jnp.where(turn == b, both[:, b * rows:(b + 1) * rows], picked)
    col_ref[...] = picked

    for d in range(1, n):

        @pl.when(me - d >= 0)
        def _():
            col_copy(d, me - d, me - d).wait_send()

        sel_copy(d, me, lax.rem(me + d, n)).wait_send()
    @pl.when(parity == 0)
    def _():
        across(0).wait_send()

    @pl.when(pair + 1 < pairs)
    def _():
        chain(0).wait_send()

    for age in range(1, pairs):

        @pl.when(pair >= age)
        def _():
            across(age).wait_send()

        if age + 1 < pairs:

            @pl.when((pair >= age) & (pair + 1 < pairs))
            def _():
                chain(age).wait_send()

    for d in range(n):
        forward(d).wait_send()
    for c in range(chunks):
        y_copy(c).wait_send()
        x_copy(c).wait_send()
        for d in range(1, quads):
            z_copy(c, d).wait_send()


def hand_over(context, scores, projected, context_out, scores_out, projected_out):
    context_out[...] = context[...]
    scores_out[...] = scores[...]
    projected_out[...] = projected[...]


def shards(
    n, queries, keys, values, hidden, norm_gain, retained_lists, counts, affine_matrix,
    affine_offset_vector,
):
    rows, query_width = queries.shape
    width = hidden.shape[1]
    depth, columns = affine_matrix.shape
    kv_width = keys.shape[1]
    group = query_width // kv_width
    half = width // n // 2
    out_rows = rows // 2
    kept_total = n * out_rows
    chunk = math.gcd(columns, 512)
    chunks = columns // chunk
    pairs = n // 2
    quads = n // 4
    lanes = max(128, rows)
    key_total = n * rows
    vmem = pl.BlockSpec(memory_space=pltpu.VMEM)
    dma = pltpu.SemaphoreType.DMA
    context, col_scores, projected = pl.pallas_call(
        functools.partial(kernel, n),
        out_shape=(
            jax.ShapeDtypeStruct((rows, query_width), F32),
            jax.ShapeDtypeStruct((1, rows), F32),
            jax.ShapeDtypeStruct((out_rows, columns), F32),
        ),
        in_specs=[
            vmem, vmem, vmem, vmem, vmem, vmem,
            pl.BlockSpec(memory_space=pltpu.SMEM),
            pl.BlockSpec(memory_space=pl.ANY),
            vmem,
        ],
        out_specs=(vmem, vmem, vmem),
        scratch_shapes=[
            pltpu.VMEM((depth, columns), BF16),
            pltpu.VMEM((n, 2, rows, kv_width), BF16),
            pltpu.VMEM((group * rows, key_total), F32),
            pltpu.VMEM((group * rows, key_total), BF16),
            pltpu.VMEM((n, rows, half), BF16),
            pltpu.VMEM((2, n, rows, half), BF16),
            pltpu.VMEM((kept_total, key_total), BF16),
            pltpu.VMEM((kept_total, 2 * half), BF16),
            pltpu.VMEM((chunks, kept_total // 2, chunk), BF16),
            pltpu.VMEM((chunks, kept_total // 2, chunk), BF16),
            pltpu.VMEM((chunks, kept_total // 2, chunk), F32),
            pltpu.VMEM((chunks, kept_total // 4, chunk), BF16),
            pltpu.VMEM((chunks, kept_total // 4, chunk), BF16),
            pltpu.VMEM((chunks, quads, out_rows, chunk), BF16),
            pltpu.VMEM((chunks, quads, out_rows, chunk), BF16),
            pltpu.VMEM((key_total // lanes, 8, lanes), F32),
            pltpu.VMEM((n, 8, lanes), F32),
            pltpu.VMEM((8, lanes), F32),
            pltpu.VMEM((8, lanes), F32),
            dma,
            dma((pairs,)), dma((pairs,)),
            dma((pairs,)), dma((pairs,)),
            dma((n,)), dma((n,)),
            dma((n,)), dma((n,)),
            dma((chunks,)), dma((chunks,)),
            dma((chunks,)), dma((chunks,)),
            dma((chunks, quads)), dma((chunks, quads)),
            dma((n,)), dma((n,)),
            dma, dma,
        ],
        compiler_params=pltpu.CompilerParams(collective_id=0, has_side_effects=True),
    )(
        queries, keys, values, hidden, norm_gain.reshape(1, width),
        retained_lists.reshape(1, rows), counts, affine_matrix,
        affine_offset_vector,
    )
    context, col_scores, projected = pl.pallas_call(
        hand_over,
        out_shape=(
            jax.ShapeDtypeStruct(context.shape, F32),
            jax.ShapeDtypeStruct(col_scores.shape, F32),
            jax.ShapeDtypeStruct(projected.shape, F32),
        ),
        in_specs=[vmem, vmem, vmem],
        out_specs=(vmem, vmem, vmem),
    )(context, col_scores, projected)
    return (context, col_scores.reshape(rows), projected)


def solution(mesh):
    in_specs = (
        P(("grp", "seq"), "ten"),
        P(("grp", "seq"), "ten"),
        P(("grp", "seq"), "ten"),
        P(("grp", "seq"), None),
        P(),
        P(("grp", "seq")),
        P("grp"),
        P("seq", "ten"),
        P("ten"),
    )
    out_specs = (P(("grp", "seq"), "ten"), P(("grp", "seq")), P(("grp", "seq"), "ten"))
    return jax.shard_map(
        functools.partial(shards, mesh.shape["seq"]),
        mesh=mesh, in_specs=in_specs, out_specs=out_specs, check_vma=False,
    )
```

```python
import functools
import math

import jax
import jax.numpy as jnp
from jax import lax
from jax.experimental import pallas as pl
from jax.experimental.pallas import tpu as pltpu
from jax.sharding import PartitionSpec as P

HEAD_SIZE = 128
QUERY_HEADS = 32
F32 = jnp.float32
BF16 = jnp.bfloat16


def remote(src, dst, send_sem, recv_sem, where):
    return pltpu.make_async_remote_copy(
        src_ref=src,
        dst_ref=dst,
        send_sem=send_sem,
        recv_sem=recv_sem,
        device_id=where,
        device_id_type=pl.DeviceIdType.MESH,
    )


def kernel(
    n,
    q_ref, k_ref, v_ref, h_ref, gain_ref, list_ref, count_ref, a_hbm, bias_ref,
    ctx_ref, col_ref, out_ref,
    a_ref, kvbuf, s_ref, e_ref, sel_send, sel_recv, g_ref, comp_ref,
    y_send, y_recv, own_ref, x_send, x_recv, z_send, z_recv, c_send, c_recv, ct_send, ct_recv,
    a_sem, kz_ssem, kz_rsem, ky_ssem, ky_rsem, sv_ssem, sv_rsem, fw_ssem, fw_rsem,
    y_ssem, y_rsem, x_ssem, x_rsem, z_ssem, z_rsem, c_ssem, c_rsem, ct_ssem, ct_rsem,
):
    me = lax.axis_index("seq")
    ten = lax.axis_index("ten")
    sibling = {"ten": 1 - ten}
    rows = q_ref.shape[0]
    key_total = n * rows
    kv_heads = k_ref.shape[1] // HEAD_SIZE
    group = q_ref.shape[1] // k_ref.shape[1]
    width = h_ref.shape[1]
    half = width // n // 2
    out_rows = out_ref.shape[0]
    chunk = y_recv.shape[2]
    chunks = y_recv.shape[0]
    pairs = n // 2
    parity = lax.rem(me, 2)
    pair = lax.div(me, 2)
    partner = {"seq": me + 1 - 2 * parity}
    quads = pairs // 2
    pair_parity = lax.rem(pair, 2)
    other_pair = pair + 1 - 2 * pair_parity

    a_copy = pltpu.make_async_copy(a_hbm, a_ref, a_sem)
    a_copy.start()
    kvbuf[...] = jnp.zeros_like(kvbuf)
    kvbuf[me, 0] = k_ref[...]
    kvbuf[me, 1] = v_ref[...]

    barrier = pltpu.get_barrier_semaphore()
    for d in range(1, n):
        pl.semaphore_signal(
            barrier, inc=1, device_id={"seq": lax.rem(me + d, n)},
            device_id_type=pl.DeviceIdType.MESH,
        )
    pl.semaphore_signal(
        barrier, inc=1, device_id=sibling, device_id_type=pl.DeviceIdType.MESH
    )
    pl.semaphore_wait(barrier, n)

    def chain(age):
        block = kvbuf.at[2 * (pair - age) + parity]
        target = {"seq": me + 2}
        return remote(block, block, kz_ssem.at[age], kz_rsem.at[age + 1], target)

    def chain_in(age):
        block = kvbuf.at[2 * (pair - age) + parity]
        return remote(block, block, kz_ssem.at[age - 1], kz_rsem.at[age], partner)

    def across(age):
        block = kvbuf.at[2 * (pair - age) + parity]
        return remote(block, block, ky_ssem.at[age], ky_rsem.at[age], partner)

    def across_in(age):
        block = kvbuf.at[2 * (pair - age) + 1 - parity]
        return remote(block, block, ky_ssem.at[age], ky_rsem.at[age], partner)

    @pl.when(pair + 1 < pairs)
    def _():
        chain(0).start()

    @pl.when(parity == 0)
    def _():
        across(0).start()

    def relay(age):
        @pl.when(pair >= age)
        def _():
            chain_in(age).wait_recv()
            across(age).start()

        if age + 1 < pairs:

            @pl.when((pair >= age) & (pair + 1 < pairs))
            def _():
                chain(age).start()

    square = jnp.zeros((rows, 1), F32)
    step = math.gcd(width, 1024)
    for c in range(width // step):
        x = h_ref[:, c * step:(c + 1) * step].astype(F32)
        square = square + jnp.sum(x * x, axis=1, keepdims=True)
    rescale = lax.rsqrt(square / width + 1e-06)
    lane = lax.broadcasted_iota(jnp.int32, (rows, rows), 1)
    line = lax.broadcasted_iota(jnp.int32, (rows, rows), 0)
    kept = jnp.sum(jnp.where(lane == line, list_ref[...], 0), axis=1, keepdims=True)
    selector = (kept == lane).astype(F32).astype(BF16)

    def chosen(owner):
        columns = pl.ds(pl.multiple_of(owner * (2 * half) + ten * half, 128), half)
        x = h_ref[:, columns].astype(F32) * rescale * gain_ref[:, columns]
        return jnp.dot(selector, x.astype(BF16), preferred_element_type=F32).astype(BF16)

    def sel_copy(d, source, target):
        return remote(
            sel_send.at[d], sel_recv.at[ten, source], sv_ssem.at[d], sv_rsem.at[d], {"seq": target}
        )

    order = sorted(range(1, n), key=lambda d: abs(2 * d - n))
    for d in order:
        owner = lax.rem(me + d, n)
        sel_send[d] = chosen(owner)
        sel_copy(d, me, owner).start()
    sel_recv[ten, me] = chosen(me)

    def forward(d):
        source = lax.rem(me - d + n, n)
        block = sel_recv.at[ten, source]
        return remote(block, block, fw_ssem.at[d], fw_rsem.at[d], sibling)

    forward(0).start()

    at = lax.broadcasted_iota(jnp.int32, (1, key_total), 1)
    place = jnp.full((1, key_total), -1, jnp.int32)
    start = jnp.int32(0)
    for s in range(n):
        t = at - s * rows
        place = jnp.where((t >= 0) & (t < count_ref[s]), start + t, place)
        start = start + count_ref[s]
    row_at = lax.broadcasted_iota(jnp.int32, (out_rows, key_total), 0)
    for side in range(2):
        side_parity = 1 - parity if side == 0 else parity
        for d in range(pairs):
            origin = other_pair if d < quads else pair
            base = (2 * lax.rem(origin + 2 * (d % quads), pairs) + side_parity) * out_rows
            first = (side * pairs + d) * out_rows
            g_ref[first:first + out_rows, :] = (
                (row_at + base == place).astype(F32).astype(BF16)
            )

    relay(1)
    for at, d in enumerate(order):
        sel_copy(d, lax.rem(me - d + n, n), me).wait_recv()
        forward(d).start()
        if at % 2 == 0 and 0 < at < n - 2:
            relay(at // 2 + 1)
    for d in range(n):
        source = lax.rem(me - d + n, n)
        block = sel_recv.at[1 - ten, source]
        remote(block, block, fw_ssem.at[d], fw_rsem.at[d], sibling).wait_recv()
    for side in range(2):
        comp_ref[:, side * half:(side + 1) * half] = jnp.dot(
            g_ref[...], sel_recv[side].reshape(key_total, half), preferred_element_type=F32
        ).astype(BF16)
    a_copy.wait()


    other = {"seq": 2 * other_pair + parity}

    def y_copy(c):
        target = other if c == 0 else partner
        return remote(y_send.at[c], y_recv.at[c], y_ssem.at[c], y_rsem.at[c], target)

    def x_copy(c):
        target = partner if c == 0 else other
        return remote(x_send.at[c], x_recv.at[c], x_ssem.at[c], x_rsem.at[c], target)

    def z_copy(c, d):
        target = {"seq": 2 * lax.rem(pair + 2 * d, pairs) + parity}
        return remote(
            z_send.at[c, d], z_recv.at[c, d], z_ssem.at[c, d], z_rsem.at[c, d], target
        )

    quad_rows = quads * out_rows

    def to_other_pair(c):
        y_copy(c).wait_recv()
        x_send[c] = (
            own_ref[c, :quad_rows, :] + y_recv[c, :quad_rows, :].astype(F32)
        ).astype(BF16)
        x_copy(c).start()

    def to_owners(c):
        x_copy(c).wait_recv()
        for d in range(quads):
            part = slice(quad_rows + d * out_rows, quad_rows + (d + 1) * out_rows)
            total = (
                own_ref[c, part, :]
                + y_recv[c, part, :].astype(F32)
                + x_recv[c, d * out_rows:(d + 1) * out_rows, :].astype(F32)
            )
            if d == 0:
                own_ref[c, part, :] = total
            else:
                z_send[c, d] = total.astype(BF16)
                z_copy(c, d).start()

    for c in range(chunks):
        columns = slice(c * chunk, (c + 1) * chunk)
        part = jnp.dot(comp_ref[...], a_ref[:, columns], preferred_element_type=F32)
        quarters = [part[i * quad_rows:(i + 1) * quad_rows] for i in range(4)]
        away, stay = ((0, 2), (1, 3)) if c == 0 else ((0, 1), (2, 3))
        for i in range(2):
            lines = slice(i * quad_rows, (i + 1) * quad_rows)
            y_send[c, lines, :] = quarters[away[i]].astype(BF16)
        y_copy(c).start()
        for i in range(2):
            own_ref[c, i * quad_rows:(i + 1) * quad_rows, :] = quarters[stay[i]]

    @pl.when(parity == 1)
    def _():
        across_in(0).wait_recv()

    for age in range(1, pairs):

        @pl.when(pair >= age)
        def _():
            across_in(age).wait_recv()

    key_pos = lax.broadcasted_iota(jnp.int32, (rows, key_total), 1)
    query_pos = me * rows + lax.broadcasted_iota(jnp.int32, (rows, key_total), 0)
    allowed = key_pos <= query_pos
    columns_total = jnp.zeros((8, key_total), F32)
    for h in range(kv_heads):
        heads = slice(h * HEAD_SIZE, (h + 1) * HEAD_SIZE)
        query = jnp.concatenate(
            [
                q_ref[:, (h * group + a) * HEAD_SIZE:(h * group + a + 1) * HEAD_SIZE]
                for a in range(group)
            ],
            axis=0,
        )
        key = kvbuf[:, 0, :, heads].reshape(key_total, HEAD_SIZE)
        value = kvbuf[:, 1, :, heads].reshape(key_total, HEAD_SIZE)
        s_ref[...] = lax.dot_general(
            query, key, (((1,), (1,)), ((), ())), preferred_element_type=F32
        )
        inverses = []
        for a in range(group):
            lines = slice(a * rows, (a + 1) * rows)
            scores = jnp.where(allowed, s_ref[lines, :] * HEAD_SIZE ** (-0.5), -1e30)
            largest = jnp.max(scores, axis=1, keepdims=True)
            weights = jnp.where(allowed, jnp.exp(scores - largest), 0.0)
            e_ref[lines, :] = weights.astype(BF16)
            inverse = 1.0 / jnp.sum(weights, axis=1, keepdims=True)
            inverses.append(inverse)
            columns_total = columns_total + jnp.sum(
                (weights * inverse).reshape(rows // 8, 8, key_total), axis=0
            )
        mixed = jnp.dot(e_ref[...], value, preferred_element_type=F32)
        for a in range(group):
            place_at = (h * group + a) * HEAD_SIZE
            ctx_ref[:, place_at:place_at + HEAD_SIZE] = (
                mixed[a * rows:(a + 1) * rows] * inverses[a]
            )
    lanes = c_send.shape[2]
    per = lanes // rows
    for b in range(n // per):
        c_send[b] = columns_total[:, b * lanes:(b + 1) * lanes]

    def col_copy(d, owner, target):
        return remote(
            c_send.at[lax.div(owner, per)], c_recv.at[d], c_ssem.at[d], c_rsem.at[d],
            {"seq": target},
        )

    for d in range(1, n):

        @pl.when(me - d >= 0)
        def _():
            col_copy(d, me - d, me - d).start()

    to_other_pair(0)
    for c in range(1, chunks):
        to_other_pair(c)
        if c > 1:
            to_owners(c - 1)
    if chunks > 1:
        to_owners(chunks - 1)
    to_owners(0)

    mine = c_send[lax.div(me, per)]
    for d in range(1, n):
        c_recv_valid = me + d < n

        @pl.when(c_recv_valid)
        def _():
            col_copy(d, me, me).wait_recv()

        @pl.when(jnp.logical_not(c_recv_valid))
        def _():
            c_recv[d] = jnp.zeros_like(c_recv[d])

        mine = mine + c_recv[d]
    ct_send[...] = mine
    ct = remote(ct_send, ct_recv, ct_ssem, ct_rsem, sibling)
    ct.start()

    for c in range(chunks):
        columns = slice(c * chunk, (c + 1) * chunk)
        total = own_ref[c, quad_rows:quad_rows + out_rows, :]
        for d in range(1, quads):
            z_copy(c, d).wait_recv()
            total = total + z_recv[c, d].astype(F32)
        out_ref[:, columns] = total + bias_ref[columns].reshape(1, chunk)

    ct.wait()
    both = jnp.sum(ct_send[...] + ct_recv[...], axis=0, keepdims=True) / QUERY_HEADS
    turn = lax.rem(me, per)
    picked = both[:, :rows]
    for b in range(1, per):
        picked = jnp.where(turn == b, both[:, b * rows:(b + 1) * rows], picked)
    col_ref[...] = picked

    for d in range(1, n):

        @pl.when(me - d >= 0)
        def _():
            col_copy(d, me - d, me - d).wait_send()

        sel_copy(d, me, lax.rem(me + d, n)).wait_send()
    @pl.when(parity == 0)
    def _():
        across(0).wait_send()

    @pl.when(pair + 1 < pairs)
    def _():
        chain(0).wait_send()

    for age in range(1, pairs):

        @pl.when(pair >= age)
        def _():
            across(age).wait_send()

        if age + 1 < pairs:

            @pl.when((pair >= age) & (pair + 1 < pairs))
            def _():
                chain(age).wait_send()

    for d in range(n):
        forward(d).wait_send()
    for c in range(chunks):
        y_copy(c).wait_send()
        x_copy(c).wait_send()
        for d in range(1, quads):
            z_copy(c, d).wait_send()


def hand_over(context, scores, projected, context_out, scores_out, projected_out):
    context_out[...] = context[...]
    scores_out[...] = scores[...]
    projected_out[...] = projected[...]


def shards(
    n, queries, keys, values, hidden, norm_gain, retained_lists, counts, affine_matrix,
    affine_offset_vector,
):
    rows, query_width = queries.shape
    width = hidden.shape[1]
    depth, columns = affine_matrix.shape
    kv_width = keys.shape[1]
    group = query_width // kv_width
    half = width // n // 2
    out_rows = rows // 2
    kept_total = n * out_rows
    chunk = math.gcd(columns, 512)
    chunks = columns // chunk
    pairs = n // 2
    quads = n // 4
    lanes = max(128, rows)
    key_total = n * rows
    vmem = pl.BlockSpec(memory_space=pltpu.VMEM)
    dma = pltpu.SemaphoreType.DMA
    context, col_scores, projected = pl.pallas_call(
        functools.partial(kernel, n),
        out_shape=(
            jax.ShapeDtypeStruct((rows, query_width), F32),
            jax.ShapeDtypeStruct((1, rows), F32),
            jax.ShapeDtypeStruct((out_rows, columns), F32),
        ),
        in_specs=[
            vmem, vmem, vmem, vmem, vmem, vmem,
            pl.BlockSpec(memory_space=pltpu.SMEM),
            pl.BlockSpec(memory_space=pl.ANY),
            vmem,
        ],
        out_specs=(vmem, vmem, vmem),
        scratch_shapes=[
            pltpu.VMEM((depth, columns), BF16),
            pltpu.VMEM((n, 2, rows, kv_width), BF16),
            pltpu.VMEM((group * rows, key_total), F32),
            pltpu.VMEM((group * rows, key_total), BF16),
            pltpu.VMEM((n, rows, half), BF16),
            pltpu.VMEM((2, n, rows, half), BF16),
            pltpu.VMEM((kept_total, key_total), BF16),
            pltpu.VMEM((kept_total, 2 * half), BF16),
            pltpu.VMEM((chunks, kept_total // 2, chunk), BF16),
            pltpu.VMEM((chunks, kept_total // 2, chunk), BF16),
            pltpu.VMEM((chunks, kept_total // 2, chunk), F32),
            pltpu.VMEM((chunks, kept_total // 4, chunk), BF16),
            pltpu.VMEM((chunks, kept_total // 4, chunk), BF16),
            pltpu.VMEM((chunks, quads, out_rows, chunk), BF16),
            pltpu.VMEM((chunks, quads, out_rows, chunk), BF16),
            pltpu.VMEM((key_total // lanes, 8, lanes), F32),
            pltpu.VMEM((n, 8, lanes), F32),
            pltpu.VMEM((8, lanes), F32),
            pltpu.VMEM((8, lanes), F32),
            dma,
            dma((pairs,)), dma((pairs,)),
            dma((pairs,)), dma((pairs,)),
            dma((n,)), dma((n,)),
            dma((n,)), dma((n,)),
            dma((chunks,)), dma((chunks,)),
            dma((chunks,)), dma((chunks,)),
            dma((chunks, quads)), dma((chunks, quads)),
            dma((n,)), dma((n,)),
            dma, dma,
        ],
        compiler_params=pltpu.CompilerParams(collective_id=0, has_side_effects=True),
    )(
        queries, keys, values, hidden, norm_gain.reshape(1, width),
        retained_lists.reshape(1, rows), counts, affine_matrix,
        affine_offset_vector,
    )
    context, col_scores, projected = pl.pallas_call(
        hand_over,
        out_shape=(
            jax.ShapeDtypeStruct(context.shape, F32),
            jax.ShapeDtypeStruct(col_scores.shape, F32),
            jax.ShapeDtypeStruct(projected.shape, F32),
        ),
        in_specs=[vmem, vmem, vmem],
        out_specs=(vmem, vmem, vmem),
    )(context, col_scores, projected)
    return (context, col_scores.reshape(rows), projected)


def solution(mesh):
    in_specs = (
        P(("grp", "seq"), "ten"),
        P(("grp", "seq"), "ten"),
        P(("grp", "seq"), "ten"),
        P(("grp", "seq"), None),
        P(),
        P(("grp", "seq")),
        P("grp"),
        P("seq", "ten"),
        P("ten"),
    )
    out_specs = (P(("grp", "seq"), "ten"), P(("grp", "seq")), P(("grp", "seq"), "ten"))
    return jax.shard_map(
        functools.partial(shards, mesh.shape["seq"]),
        mesh=mesh, in_specs=in_specs, out_specs=out_specs, check_vma=False,
    )
```
